32 devices in a mesh: ka: 8 (over y, x, core), ga: 4 (over z).
Axes of the slice: x: 2, y: 2, z: 4, core: 2. Of those that a mesh axis runs over, the one named last changes fastest.
Arguments:
- orbitals: bfloat16 [2, 8, 2, 16, 256], P(None, 'ka'), may hold values from -4 to 4
- fit_vectors: bfloat16 [2, 256, 12288], P(None, None, 'ga'), may hold values from -0.375 to 0.375
- screening: float32 [8, 2, 12288], P('ka', None, 'ga'), may hold values from 0.005 to 0.05
- qpoint_table: int32 [2, 2], replicated, may hold values from 0 to 1, as said below
Outputs:
- kernel: float32 [2, 3, 8, 128, 128], P(None, None, 'ka', 'ga')
The draws below stay inside these ranges and needn't reach their ends.
Inputs may be any that keep to these rules, and one draw needn't show every extreme that they name: qpoint_table[a, b] depends only on (a - b) mod 2.
All inputs are finite; a program needn't handle non-finite values.
Results may differ from the reference program's by a relative error of at most 0.0042.
Values may be sent and summed in bfloat16 or wider, within the bound.
A program may use at most 128 MiB of HBM per device.

```python
import math
import jax
import jax.numpy as jnp
from jax import lax

NV = 8
NB = 16
NMU = 256
NG = 12288
NKY = 2
STEPS = 3
NKX = 8


def draw_qpoint_table(key, part):
    value_key = jax.random.fold_in(key, 11)
    place_key = jax.random.fold_in(key, 12)
    stored = jax.random.randint(value_key, (NKY,), 0, NKY).astype(jnp.int32)
    places_drawn = jax.random.permutation(place_key, NKY).astype(jnp.int32)
    stored = stored.at[places_drawn[0]].set(0)
    stored = stored.at[places_drawn[1]].set(NKY - 1)
    places = jnp.arange(NKY, dtype=jnp.int32)
    return stored[(places[:, None] - places[None, :]) % NKY].astype(jnp.int32)


def steps_of(key, shape, shards, low, top_value):
    gain = 1.0
    for axis_at, shards_of in shards:
        draws = jax.random.uniform(jax.random.fold_in(jax.random.fold_in(key, 6), axis_at), (shards_of,), jnp.float32, low / len(shards), top_value / len(shards))
        gain = gain * jnp.repeat(jnp.exp(draws), shape[axis_at] // shards_of).reshape((-1,) + (1,) * (len(shape) - 1 - axis_at))
    return gain


def bell_draw(stream_key, shape, scale, limit, pieces=(), kind=jnp.bfloat16):
    drawn = jax.random.normal(stream_key, shape, jnp.float32) * scale
    if len(pieces) > 0:
        drawn = steps_of(stream_key, shape, pieces, -0.22, 0.18) * drawn
    return jnp.clip(drawn, min=-limit, max=limit).astype(kind)


def setup_inputs(seed: int = 0) -> dict:
    key_list = jax.random.split(jax.random.key(seed), 5)
    return {
        "orbitals": bell_draw(key_list[0], (2, NKX, NKY, NB, NMU), 0.5, 4.0, ((1, 8),)),
        "fit_vectors": bell_draw(key_list[1], (2, NMU, NG), NMU ** -0.5, 0.375, ((2, 4),)),
        "screening": jnp.clip(jnp.exp(math.log(0.05) - 2.3025851 * jax.random.uniform(key_list[2], (NKX, NKY, NG), jnp.float32) ** steps_of(key_list[2], (NKX, NKY, NG), ((0, 8), (2, 4)), -0.2, 0.2)), 0.005, 0.05),
        "qpoint_table": draw_qpoint_table(jax.random.fold_in(key_list[4], 71), 0),
    }


def densities(first_band, second_band, fit_vectors):
    points = first_band.shape[-1]
    first_real = first_band[0].astype(jnp.float32)[:, :, None, None, :]
    first_imag = first_band[1].astype(jnp.float32)[:, :, None, None, :]
    second_real = second_band[0].astype(jnp.float32)[None, None, :, :, :]
    second_imag = second_band[1].astype(jnp.float32)[None, None, :, :, :]
    pair_real = (first_real * second_real + first_imag * second_imag).astype(jnp.bfloat16).reshape(-1, points)
    pair_imag = (first_real * second_imag - first_imag * second_real).astype(jnp.bfloat16).reshape(-1, points)
    density_real = jnp.dot(pair_real, fit_vectors[0], preferred_element_type=jnp.float32) - jnp.dot(pair_imag, fit_vectors[1], preferred_element_type=jnp.float32)
    density_imag = jnp.dot(pair_real, fit_vectors[1], preferred_element_type=jnp.float32) + jnp.dot(pair_imag, fit_vectors[0], preferred_element_type=jnp.float32)
    return density_real.astype(jnp.bfloat16), density_imag.astype(jnp.bfloat16)


def mixing(first, second):
    return jnp.einsum("abdeg,ahdig->abhdei", first.astype(jnp.float32), second.astype(jnp.float32))


def kernel_block(home_orbitals, far_orbitals, fit_vectors, pair_screen):
    kys = home_orbitals.shape[1]
    valence = NV
    conduct = home_orbitals.shape[2] - valence
    width = fit_vectors.shape[2]
    cond_real, cond_imag = densities(home_orbitals[:, :, valence:], far_orbitals[:, :, valence:], fit_vectors)
    val_real, val_imag = densities(home_orbitals[:, :, :valence], far_orbitals[:, :, :valence], fit_vectors)
    cond_real = cond_real.reshape(kys, conduct, kys, conduct, width)
    cond_imag = cond_imag.reshape(kys, conduct, kys, conduct, width)
    screen_wide = pair_screen[:, None, :, None, :]
    weight_real = (val_real.reshape(kys, valence, kys, valence, width).astype(jnp.float32) * screen_wide).astype(jnp.bfloat16)
    weight_imag = (val_imag.reshape(kys, valence, kys, valence, width).astype(jnp.float32) * screen_wide).astype(jnp.bfloat16)
    kernel_real = mixing(cond_real, weight_real) + mixing(cond_imag, weight_imag)
    kernel_imag = mixing(cond_real, weight_imag) - mixing(cond_imag, weight_real)
    row_count = kys * conduct * valence
    return jnp.stack([kernel_real.reshape(row_count, row_count), kernel_imag.reshape(row_count, row_count)], 0)


def reference(orbitals, fit_vectors, screening, qpoint_table):
    by_row = jnp.moveaxis(orbitals, 1, 0)
    outputs = []
    for distance in range(1, STEPS + 1):
        far_rows = jnp.roll(by_row, distance, axis=0)
        pair_screen = jnp.take(screening[distance], qpoint_table, axis=0)
        blocks = lax.map(lambda rows_pair: kernel_block(rows_pair[0], rows_pair[1], fit_vectors, pair_screen), (by_row, far_rows))
        outputs.append(jnp.moveaxis(blocks, 0, 1))
    return jnp.stack(outputs, 1)
```

```python
import functools
import jax
import jax.numpy as jnp
from jax import lax
from jax.experimental import pallas as pl
from jax.experimental.pallas import tpu as pltpu
from jax.sharding import PartitionSpec as P

NV = 8
STEPS = 3
MESH = pl.DeviceIdType.MESH
LINK = jnp.bfloat16


def dot_nt(a, b):
    return lax.dot_general(a, b, (((1,), (1,)), ((), ())), preferred_element_type=jnp.float32)


def pairs(ar, ai, br, bi):
    rows = ar.shape[0] * br.shape[0]
    ar, ai, br, bi = ar[:, None, :], ai[:, None, :], br[None], bi[None]
    real = (ar * br + ai * bi).reshape(rows, -1)
    imag = (ar * bi - ai * br).reshape(rows, -1)
    return real, imag


def swapped(x, size):
    row = lax.broadcasted_iota(jnp.int32, x.shape, 0)
    lane = lax.broadcasted_iota(jnp.int32, x.shape, 1)
    d = 1
    while d < size:
        rb = lax.rem(lax.div(row, d), 2)
        lb = lax.rem(lax.div(lane, d * size), 2)
        up = pltpu.roll(pltpu.roll(x, x.shape[0] - d, 0), d * size, 1)
        down = pltpu.roll(pltpu.roll(x, d, 0), x.shape[1] - d * size, 1)
        x = jnp.where(rb == lb, x, jnp.where(rb == 0, up, down))
        d *= 2
    return x


def kernel(n, ng, tile, orb_in, fit_in, scr_in, tab_in, out, orb, fit, mix, own_scr, sel, scr, p1, p2, pv,
           kf, kb, rb, tab, tab_sem, own_sem, fit_sem, orb_send, orb_recv, scr_send, scr_recv, out_send, out_recv):
    me, g = lax.axis_index("ka"), lax.axis_index("ga")
    e = lax.rem(me, 2)
    base = me - e
    width = fit_in.shape[2]
    tiles = width // tile
    bands = orb_in.shape[3]
    cond = bands - NV
    half = cond * cond

    barrier = pltpu.get_barrier_semaphore()
    count = 0
    for j in range(1, n):
        pl.semaphore_signal(barrier, inc=1, device_id=(lax.rem(me + j, n), g), device_id_type=MESH)
        count += 1
    for dg in range(ng - 1, 0, -1):
        for di in range(2):
            there = (base + lax.rem(e + di, 2), lax.rem(g + dg, ng))
            pl.semaphore_signal(barrier, inc=1, device_id=there, device_id_type=MESH)
            count += 1

    tab_copy = pltpu.make_async_copy(tab_in, tab, tab_sem)
    own_copy = pltpu.make_async_copy(scr_in.at[0], own_scr, own_sem)
    tab_copy.start()
    own_copy.start()
    fits = []
    for t in range(tiles):
        part = pl.ds(t * tile, tile)
        copy = pltpu.make_async_copy(fit_in.at[:, :, part], fit.at[:, :, part], fit_sem.at[t])
        copy.start()
        fits.append(copy)

    tab_copy.wait()
    own_copy.wait()
    for p in range(sel.shape[0]):
        row = jnp.zeros((1, width), jnp.float32)
        for q in range(own_scr.shape[0]):
            row = row + jnp.where(tab[p, 0] == q, 1.0, 0.0) * own_scr[q:q + 1]
        lines = [row[:, c * 128:(c + 1) * 128] for c in range(width // 128)]
        lines.append(jnp.zeros((sel.shape[1] - width // 128, 128), jnp.float32))
        sel[p] = jnp.concatenate([x for x in lines if x.shape[0]], 0).astype(LINK)
    pl.semaphore_wait(barrier, count)

    def screen_copy(s, j):
        return pltpu.make_async_remote_copy(
            src_ref=sel.at[lax.rem(e + j, 2)], dst_ref=scr.at[s], send_sem=scr_send.at[j - 1],
            recv_sem=scr_recv.at[s], device_id=(lax.rem(me + j, n), g), device_id_type=MESH)

    for s in range(STEPS):
        @pl.when(me == s + 1)
        def _():
            for j in range(1, n):
                screen_copy(s, j).start()
            pltpu.make_async_copy(sel.at[e], scr.at[s], scr_recv.at[s]).start()

    def orb_copy(h, d):
        there = lax.rem(base + 2 * h + d + n, n)
        return pltpu.make_async_remote_copy(
            src_ref=orb_in.at[:, 0], dst_ref=orb.at[2 * h + 1 - e], send_sem=orb_send.at[h, d],
            recv_sem=orb_recv.at[2 * h + 1 - e], device_id=(there, g), device_id_type=MESH)

    sends = [(h, d) for h in (1, 0, *range(2, (STEPS + 1) // 2 + 1)) for d in range(2)]

    def each_orb(act):
        for h, d in sends:
            if h == 0:
                @pl.when(e != d)
                def _():
                    act(orb_copy(h, d))
            else:
                @pl.when(2 * h + 1 - e <= STEPS + 1)
                def _():
                    act(orb_copy(h, d))

    each_orb(lambda c: c.start())
    pltpu.make_async_copy(orb_in.at[:, 0], orb.at[1 - e], orb_recv.at[1 - e]).start()

    for t in range(tiles):
        fits[t].wait()
        part = slice(t * tile, (t + 1) * tile)
        x, y = fit[0, :, part].astype(jnp.float32), fit[1, :, part].astype(jnp.float32)
        mix[t, :, :tile] = (x + y).astype(jnp.bfloat16)
        mix[t, :, tile:] = (y - x).astype(jnp.bfloat16)

    def pair_products(s):
        for i in range(2):
            for a in range(2):
                b = lax.rem(a + e, 2)
                k = 2 * i + a
                home = orb[1 - i, :, a].astype(jnp.float32)
                far = orb[2 - i + s, :, b].astype(jnp.float32)
                cr, ci = pairs(home[0, NV:], home[1, NV:], far[0, NV:], far[1, NV:])
                both, less = (cr + ci).astype(jnp.bfloat16), (cr - ci).astype(jnp.bfloat16)
                low, high = slice(k * half, (k + 1) * half), slice((4 + k) * half, (5 + k) * half)
                p1[s, low], p1[s, high] = both, less
                p2[s, low], p2[s, high] = less, -both
                vr, vi = pairs(home[0, :NV], home[1, :NV], far[0, :NV], far[1, :NV])
                vr, vi = vr.astype(jnp.bfloat16), vi.astype(jnp.bfloat16)
                pv[s, k] = jnp.concatenate(
                    [jnp.concatenate([vr, -vi], 1), jnp.concatenate([vi, vr], 1)], 0)

    def out_copy(s, di, dg):
        i, gt = lax.rem(e + di, 2), lax.rem(g + dg, ng)
        return pltpu.make_async_remote_copy(
            src_ref=kb.at[s, i, gt], dst_ref=rb.at[s, di, dg], send_sem=out_send.at[s, di, dg],
            recv_sem=out_recv.at[s, di, dg], device_id=(base + i, gt), device_id_type=MESH)

    moves = [(di, dg) for dg in range(ng - 1, -1, -1) for di in range(2) if di or dg]
    def fold(s, t):
        part = slice(t * tile, (t + 1) * tile)
        each = tile // 128
        lines = scr[s].astype(jnp.float32)
        screen = jnp.concatenate([lines[t * each + c:t * each + c + 1] for c in range(each)], 1)
        xw = (fit[0, :, part].astype(jnp.float32) * screen).astype(jnp.bfloat16)
        yw = (fit[1, :, part].astype(jnp.float32) * screen).astype(jnp.bfloat16)
        return dot_nt(jnp.concatenate([xw, yw], 1), mix[t])

    def screen_wait(s):
        pltpu.make_async_copy(sel.at[e], scr.at[s], scr_recv.at[s]).wait()

    def folded(s):
        total = fold(s, 0)
        for t in range(1, tiles):
            total = total + fold(s, t)
        return (total * 0.5).astype(jnp.bfloat16)

    def finish(s, total):
        u = (jnp.dot(p1[s], total, preferred_element_type=jnp.float32) + dot_nt(p2[s], total)).astype(jnp.bfloat16)
        for i in range(2):
            block = []
            for k in (2 * i, 2 * i + 1):
                mine = [u[k * half:(k + 1) * half], u[(4 + k) * half:(5 + k) * half]]
                block.append(dot_nt(jnp.concatenate(mine, 1), pv[s, k]))
            block = jnp.concatenate(block, 0).reshape(kf.shape[2:])
            kf[s, i] = block
            kb[s, i] = block.astype(LINK)
        for t in range(ng - 1):
            up = jnp.where(t >= g, t + 1, t)
            down = jnp.where(ng - 1 - t <= g, ng - 2 - t, ng - 1 - t)
            gt = jnp.where(2 * g >= ng, up, down)
            dg = lax.rem(gt - g + ng, ng)
            for di in range(2):
                out_copy(s, di, dg).start()
        out_copy(s, 1, 0).start()

    order = [*range(1, STEPS), 0]
    landed = set()

    def need(s):
        for j in sorted({0, 1, s + 1, s + 2} - landed):
            pltpu.make_async_copy(orb_in.at[:, 0], orb.at[j], orb_recv.at[j]).wait()
            landed.add(j)

    screen_wait(order[0])
    total = folded(order[0])
    for p, s in enumerate(order):
        need(s)
        pair_products(s)
        if p + 1 < STEPS:
            screen_wait(order[p + 1])
            later = folded(order[p + 1])
        finish(s, total)
        total = later

    rows = kf.shape[3]
    a_here = lax.div(g * rows, half)
    first = lax.rem(a_here + e, 2) == 0
    lane = lax.broadcasted_iota(jnp.int32, (rows, kf.shape[4]), 1)
    mid = kf.shape[4] // 2
    low = lane < mid
    for s in order:
        for di, dg in moves:
            out_copy(s, di, dg).wait_recv()
        own = kf[s, e, g]
        for dg in range(1, ng):
            own = own + rb[s, 0, dg].astype(jnp.float32)
        other = rb[s, 1, 0].astype(jnp.float32)
        for dg in range(1, ng):
            other = other + rb[s, 1, dg].astype(jnp.float32)
        b0 = jnp.where(first, own, other)
        b1 = jnp.where(first, other, own)
        out[0, s] = swapped(jnp.where(low, b0, pltpu.roll(b1, mid, 1)), NV)
        out[1, s] = swapped(jnp.where(low, pltpu.roll(b0, mid, 1), b1), NV)

    for s in range(STEPS):
        for di, dg in moves:
            out_copy(s, di, dg).wait_send()
    each_orb(lambda c: c.wait_send())
    for s in range(STEPS):
        @pl.when(me == s + 1)
        def _():
            for j in range(1, n):
                screen_copy(s, j).wait_send()


def body(orbitals, fit_vectors, screening, qpoint_table):
    n, ng = lax.axis_size("ka"), lax.axis_size("ga")
    _, _, kys, bands, points = orbitals.shape
    width = fit_vectors.shape[2]
    cond = bands - NV
    assert kys == 2 and cond == NV and n % 2 == 0 and n >= 2 * ((STEPS + 1) // 2 + 1)
    tile = next(t for t in (512, 384, 256, 128) if width % t == 0)
    rows = kys * cond * cond // ng
    wide = 2 * NV * NV
    lines = -(-width // 2048) * 16
    dma = pltpu.SemaphoreType.DMA
    any_spec = pl.BlockSpec(memory_space=pl.ANY)
    shares = pl.pallas_call(
        functools.partial(kernel, n, ng, tile),
        out_shape=pltpu.VMEM((2, STEPS, rows, wide), jnp.float32),
        in_specs=[any_spec] * 4,
        out_specs=pl.BlockSpec(memory_space=pltpu.VMEM),
        scratch_shapes=[
            pltpu.VMEM((STEPS + 2, 2, kys, bands, points), jnp.bfloat16),
            pltpu.VMEM((2, points, width), jnp.bfloat16),
            pltpu.VMEM((width // tile, points, 2 * tile), jnp.bfloat16),
            pltpu.VMEM((kys, width), jnp.float32),
            pltpu.VMEM((kys, lines, 128), LINK),
            pltpu.VMEM((STEPS, lines, 128), LINK),
            pltpu.VMEM((STEPS, 8 * cond * cond, points), jnp.bfloat16),
            pltpu.VMEM((STEPS, 8 * cond * cond, points), jnp.bfloat16),
            pltpu.VMEM((STEPS, 4, wide, 2 * points), jnp.bfloat16),
            pltpu.VMEM((STEPS, 2, ng, rows, wide), jnp.float32),
            pltpu.VMEM((STEPS, 2, ng, rows, wide), LINK),
            pltpu.VMEM((STEPS, 2, ng, rows, wide), LINK),
            pltpu.SMEM((kys, kys), jnp.int32),
            dma,
            dma,
            dma((width // tile,)),
            dma(((STEPS + 1) // 2 + 1, 2)),
            dma((STEPS + 2,)),
            dma((n - 1,)),
            dma((STEPS,)),
            dma((STEPS, 2, ng)),
            dma((STEPS, 2, ng)),
        ],
        compiler_params=pltpu.CompilerParams(collective_id=0, has_side_effects=True),
    )(orbitals, fit_vectors, screening, qpoint_table)
    return shares[:, :, None]


def solution(mesh):
    in_specs = (P(None, "ka", None, None, None), P(None, None, "ga"), P("ka", None, "ga"), P())
    out_specs = P(None, None, "ka", "ga", None)
    return jax.shard_map(body, mesh=mesh, in_specs=in_specs, out_specs=out_specs, check_vma=False)
```

```python
import functools
import jax
import jax.numpy as jnp
from jax import lax
from jax.experimental import pallas as pl
from jax.experimental.pallas import tpu as pltpu
from jax.sharding import PartitionSpec as P

NV = 8
STEPS = 3
MESH = pl.DeviceIdType.MESH
LINK = jnp.bfloat16


def dot_nt(a, b):
    return lax.dot_general(a, b, (((1,), (1,)), ((), ())), preferred_element_type=jnp.float32)


def pairs(ar, ai, br, bi):
    rows = ar.shape[0] * br.shape[0]
    ar, ai, br, bi = ar[:, None, :], ai[:, None, :], br[None], bi[None]
    real = (ar * br + ai * bi).reshape(rows, -1)
    imag = (ar * bi - ai * br).reshape(rows, -1)
    return real, imag


def swapped(x, size):
    row = lax.broadcasted_iota(jnp.int32, x.shape, 0)
    lane = lax.broadcasted_iota(jnp.int32, x.shape, 1)
    d = 1
    while d < size:
        rb = lax.rem(lax.div(row, d), 2)
        lb = lax.rem(lax.div(lane, d * size), 2)
        up = pltpu.roll(pltpu.roll(x, x.shape[0] - d, 0), d * size, 1)
        down = pltpu.roll(pltpu.roll(x, d, 0), x.shape[1] - d * size, 1)
        x = jnp.where(rb == lb, x, jnp.where(rb == 0, up, down))
        d *= 2
    return x


def kernel(n, ng, tile, orb_in, fit_in, scr_in, tab_in, out, orb, fit, mix, own_scr, sel, scr, p1, p2, pv,
           kf, kb, rb, tab, tab_sem, own_sem, fit_sem, orb_send, orb_recv, scr_send, scr_recv, out_send, out_recv):
    me, g = lax.axis_index("ka"), lax.axis_index("ga")
    e = lax.rem(me, 2)
    base = me - e
    width = fit_in.shape[2]
    tiles = width // tile
    bands = orb_in.shape[3]
    cond = bands - NV
    half = cond * cond

    barrier = pltpu.get_barrier_semaphore()
    count = 0
    for j in range(1, n):
        pl.semaphore_signal(barrier, inc=1, device_id=(lax.rem(me + j, n), g), device_id_type=MESH)
        count += 1
    for dg in range(ng - 1, 0, -1):
        for di in range(2):
            there = (base + lax.rem(e + di, 2), lax.rem(g + dg, ng))
            pl.semaphore_signal(barrier, inc=1, device_id=there, device_id_type=MESH)
            count += 1

    tab_copy = pltpu.make_async_copy(tab_in, tab, tab_sem)
    own_copy = pltpu.make_async_copy(scr_in.at[0], own_scr, own_sem)
    tab_copy.start()
    own_copy.start()
    fits = []
    for t in range(tiles):
        part = pl.ds(t * tile, tile)
        copy = pltpu.make_async_copy(fit_in.at[:, :, part], fit.at[:, :, part], fit_sem.at[t])
        copy.start()
        fits.append(copy)

    tab_copy.wait()
    own_copy.wait()
    for p in range(sel.shape[0]):
        row = jnp.zeros((1, width), jnp.float32)
        for q in range(own_scr.shape[0]):
            row = row + jnp.where(tab[p, 0] == q, 1.0, 0.0) * own_scr[q:q + 1]
        lines = [row[:, c * 128:(c + 1) * 128] for c in range(width // 128)]
        lines.append(jnp.zeros((sel.shape[1] - width // 128, 128), jnp.float32))
        sel[p] = jnp.concatenate([x for x in lines if x.shape[0]], 0).astype(LINK)
    pl.semaphore_wait(barrier, count)

    def screen_copy(s, j):
        return pltpu.make_async_remote_copy(
            src_ref=sel.at[lax.rem(e + j, 2)], dst_ref=scr.at[s], send_sem=scr_send.at[j - 1],
            recv_sem=scr_recv.at[s], device_id=(lax.rem(me + j, n), g), device_id_type=MESH)

    for s in range(STEPS):
        @pl.when(me == s + 1)
        def _():
            for j in range(1, n):
                screen_copy(s, j).start()
            pltpu.make_async_copy(sel.at[e], scr.at[s], scr_recv.at[s]).start()

    def orb_copy(h, d):
        there = lax.rem(base + 2 * h + d + n, n)
        return pltpu.make_async_remote_copy(
            src_ref=orb_in.at[:, 0], dst_ref=orb.at[2 * h + 1 - e], send_sem=orb_send.at[h, d],
            recv_sem=orb_recv.at[2 * h + 1 - e], device_id=(there, g), device_id_type=MESH)

    sends = [(h, d) for h in (1, 0, *range(2, (STEPS + 1) // 2 + 1)) for d in range(2)]

    def each_orb(act, soon, late):
        for h, d in sends:
            if h == 0:
                go = e != d
            elif h == 1:
                go = None
            else:
                go = 2 * h + 1 - e <= STEPS + 1
            first = (e == 1) if h == 1 else h == 0
            if h == 1:
                go = first if soon and not late else jnp.logical_not(first) if late and not soon else e >= 0
            elif (h == 0 and not soon) or (h > 1 and not late):
                continue

            @pl.when(go)
            def _():
                act(orb_copy(h, d))

    each_orb(lambda c: c.start(), True, False)
    pltpu.make_async_copy(orb_in.at[:, 0], orb.at[1 - e], orb_recv.at[1 - e]).start()

    for t in range(tiles):
        fits[t].wait()
        part = slice(t * tile, (t + 1) * tile)
        x, y = fit[0, :, part].astype(jnp.float32), fit[1, :, part].astype(jnp.float32)
        mix[t, :, :tile] = (x + y).astype(jnp.bfloat16)
        mix[t, :, tile:] = (y - x).astype(jnp.bfloat16)
    each_orb(lambda c: c.start(), False, True)

    def pair_products(s):
        for i in range(2):
            for a in range(2):
                b = lax.rem(a + e, 2)
                k = 2 * i + a
                home = orb[1 - i, :, a].astype(jnp.float32)
                far = orb[2 - i + s, :, b].astype(jnp.float32)
                cr, ci = pairs(home[0, NV:], home[1, NV:], far[0, NV:], far[1, NV:])
                both, less = (cr + ci).astype(jnp.bfloat16), (cr - ci).astype(jnp.bfloat16)
                low, high = slice(k * half, (k + 1) * half), slice((4 + k) * half, (5 + k) * half)
                p1[s, low], p1[s, high] = both, less
                p2[s, low], p2[s, high] = less, -both
                vr, vi = pairs(home[0, :NV], home[1, :NV], far[0, :NV], far[1, :NV])
                vr, vi = vr.astype(jnp.bfloat16), vi.astype(jnp.bfloat16)
                pv[s, i, 2 * a * half:(2 * a + 1) * half] = vr
                pv[s, i, (2 * a + 1) * half:(2 * a + 2) * half] = vi

    def out_copy(s, di, dg):
        i, gt = lax.rem(e + di, 2), lax.rem(g + dg, ng)
        return pltpu.make_async_remote_copy(
            src_ref=kb.at[s, i, gt], dst_ref=rb.at[s, di, dg], send_sem=out_send.at[s, di, dg],
            recv_sem=out_recv.at[s, di, dg], device_id=(base + i, gt), device_id_type=MESH)

    moves = [(di, dg) for dg in range(ng - 1, -1, -1) for di in range(2) if di or dg]
    def fold(s, t):
        part = slice(t * tile, (t + 1) * tile)
        each = tile // 128
        lines = scr[s].astype(jnp.float32)
        screen = jnp.concatenate([lines[t * each + c:t * each + c + 1] for c in range(each)], 1)
        xw = (fit[0, :, part].astype(jnp.float32) * screen).astype(jnp.bfloat16)
        yw = (fit[1, :, part].astype(jnp.float32) * screen).astype(jnp.bfloat16)
        return dot_nt(jnp.concatenate([xw, yw], 1), mix[t])

    def screen_wait(s):
        pltpu.make_async_copy(sel.at[e], scr.at[s], scr_recv.at[s]).wait()

    def folded(s, first, last, total=None):
        for t in range(first, last):
            total = fold(s, t) if total is None else total + fold(s, t)
        return (total * 0.5).astype(jnp.bfloat16) if last == tiles else total

    def applied(s, total):
        return (jnp.dot(p1[s], total, preferred_element_type=jnp.float32) + dot_nt(p2[s], total)).astype(jnp.bfloat16)

    sign = jnp.where(lax.broadcasted_iota(jnp.int32, (1, 2 * half), 1) < half, -1.0, 1.0)

    def finish(s, u):
        for i in range(2):
            ends = slice(2 * i * half, (2 * i + 2) * half), slice((2 * i + 4) * half, (2 * i + 6) * half)
            mixed = dot_nt(jnp.concatenate([u[ends[0]], u[ends[1]]], 0), pv[s, i])
            block = []
            for a in range(2):
                cols = slice(2 * a * half, (2 * a + 2) * half)
                by_imag = pltpu.roll(mixed[(2 + a) * half:(3 + a) * half, cols], half, 1)
                block.append(mixed[a * half:(a + 1) * half, cols] + by_imag * sign)
            block = jnp.concatenate(block, 0).reshape(kf.shape[2:])
            kf[s, i] = block
            kb[s, i] = block.astype(LINK)
        for t in range(ng - 1):
            up = jnp.where(t >= g, t + 1, t)
            down = jnp.where(ng - 1 - t <= g, ng - 2 - t, ng - 1 - t)
            gt = jnp.where(2 * g >= ng, up, down)
            dg = lax.rem(gt - g + ng, ng)
            for di in range(2):
                out_copy(s, di, dg).start()
        out_copy(s, 1, 0).start()

    order = range(STEPS)
    landed = set()

    def need(s):
        for j in sorted({0, 1, s + 1, s + 2} - landed):
            pltpu.make_async_copy(orb_in.at[:, 0], orb.at[j], orb_recv.at[j]).wait()
            landed.add(j)

    for s in order:
        screen_wait(s)
    need(order[0])
    total = folded(order[0], 0, tiles)
    pair_products(order[0])
    for p, s in enumerate(order):
        cut = min(3, tiles) if p == 0 else 1
        later = None
        if p + 1 < STEPS and cut:
            later = folded(order[p + 1], 0, cut)
        u = applied(s, total)
        if p + 1 < STEPS and cut < tiles:
            later = folded(order[p + 1], cut, tiles, later)
        finish(s, u)
        total = later
        if p == 0:
            for later_s in order[1:]:
                need(later_s)
            for later_s in order[1:]:
                pair_products(later_s)

    rows = kf.shape[3]
    a_here = lax.div(g * rows, half)
    first = lax.rem(a_here + e, 2) == 0
    lane = lax.broadcasted_iota(jnp.int32, (rows, kf.shape[4]), 1)
    mid = kf.shape[4] // 2
    low = lane < mid
    for p, s in enumerate(order):
        if p == STEPS - 1:
            each_orb(lambda c: c.wait_send(), True, True)
            for q in range(STEPS):
                @pl.when(me == q + 1)
                def _():
                    for j in range(1, n):
                        screen_copy(q, j).wait_send()
            for q in order[:-1]:
                for di, dg in moves:
                    out_copy(q, di, dg).wait_send()
        for di, dg in moves:
            out_copy(s, di, dg).wait_recv()
        own = kf[s, e, g]
        for dg in range(1, ng):
            own = own + rb[s, 0, dg].astype(jnp.float32)
        other = rb[s, 1, 0].astype(jnp.float32)
        for dg in range(1, ng):
            other = other + rb[s, 1, dg].astype(jnp.float32)
        b0 = jnp.where(first, own, other)
        b1 = jnp.where(first, other, own)
        out[0, s] = swapped(jnp.where(low, b0, pltpu.roll(b1, mid, 1)), NV)
        out[1, s] = swapped(jnp.where(low, pltpu.roll(b0, mid, 1), b1), NV)

    for di, dg in moves:
        out_copy(order[-1], di, dg).wait_send()


def body(orbitals, fit_vectors, screening, qpoint_table):
    n, ng = lax.axis_size("ka"), lax.axis_size("ga")
    _, _, kys, bands, points = orbitals.shape
    width = fit_vectors.shape[2]
    cond = bands - NV
    assert kys == 2 and cond == NV and n % 2 == 0 and n >= 2 * ((STEPS + 1) // 2 + 1)
    tile = next(t for t in (512, 384, 256, 128) if width % t == 0)
    rows = kys * cond * cond // ng
    wide = 2 * NV * NV
    lines = -(-width // 2048) * 16
    dma = pltpu.SemaphoreType.DMA
    any_spec = pl.BlockSpec(memory_space=pl.ANY)
    shares = pl.pallas_call(
        functools.partial(kernel, n, ng, tile),
        out_shape=pltpu.VMEM((2, STEPS, rows, wide), jnp.float32),
        in_specs=[any_spec] * 4,
        out_specs=pl.BlockSpec(memory_space=pltpu.VMEM),
        scratch_shapes=[
            pltpu.VMEM((STEPS + 2, 2, kys, bands, points), jnp.bfloat16),
            pltpu.VMEM((2, points, width), jnp.bfloat16),
            pltpu.VMEM((width // tile, points, 2 * tile), jnp.bfloat16),
            pltpu.VMEM((kys, width), jnp.float32),
            pltpu.VMEM((kys, lines, 128), LINK),
            pltpu.VMEM((STEPS, lines, 128), LINK),
            pltpu.VMEM((STEPS, 8 * cond * cond, points), jnp.bfloat16),
            pltpu.VMEM((STEPS, 8 * cond * cond, points), jnp.bfloat16),
            pltpu.VMEM((STEPS, 2, 2 * wide, points), jnp.bfloat16),
            pltpu.VMEM((STEPS, 2, ng, rows, wide), jnp.float32),
            pltpu.VMEM((STEPS, 2, ng, rows, wide), LINK),
            pltpu.VMEM((STEPS, 2, ng, rows, wide), LINK),
            pltpu.SMEM((kys, kys), jnp.int32),
            dma,
            dma,
            dma((width // tile,)),
            dma(((STEPS + 1) // 2 + 1, 2)),
            dma((STEPS + 2,)),
            dma((n - 1,)),
            dma((STEPS,)),
            dma((STEPS, 2, ng)),
            dma((STEPS, 2, ng)),
        ],
        compiler_params=pltpu.CompilerParams(collective_id=0, has_side_effects=True),
    )(orbitals, fit_vectors, screening, qpoint_table)
    return shares[:, :, None]


def solution(mesh):
    in_specs = (P(None, "ka", None, None, None), P(None, None, "ga"), P("ka", None, "ga"), P())
    out_specs = P(None, None, "ka", "ga", None)
    return jax.shard_map(body, mesh=mesh, in_specs=in_specs, out_specs=out_specs, check_vma=False)
```

```python
import functools
import jax
import jax.numpy as jnp
from jax import lax
from jax.experimental import pallas as pl
from jax.experimental.pallas import tpu as pltpu
from jax.sharding import PartitionSpec as P

NV = 8
STEPS = 3
MESH = pl.DeviceIdType.MESH
LINK = jnp.bfloat16


def dot_nt(a, b):
    return lax.dot_general(a, b, (((1,), (1,)), ((), ())), preferred_element_type=jnp.float32)


def pairs(ar, ai, br, bi):
    rows = ar.shape[0] * br.shape[0]
    ar, ai, br, bi = ar[:, None, :], ai[:, None, :], br[None], bi[None]
    real = (ar * br + ai * bi).reshape(rows, -1)
    imag = (ar * bi - ai * br).reshape(rows, -1)
    return real, imag


def swapped(x, size):
    row = lax.broadcasted_iota(jnp.int32, x.shape, 0)
    lane = lax.broadcasted_iota(jnp.int32, x.shape, 1)
    d = 1
    while d < size:
        rb = lax.rem(lax.div(row, d), 2)
        lb = lax.rem(lax.div(lane, d * size), 2)
        up = pltpu.roll(pltpu.roll(x, x.shape[0] - d, 0), d * size, 1)
        down = pltpu.roll(pltpu.roll(x, d, 0), x.shape[1] - d * size, 1)
        x = jnp.where(rb == lb, x, jnp.where(rb == 0, up, down))
        d *= 2
    return x


def kernel(n, ng, tile, orb_in, fit_in, scr_in, tab_in, out, orb, fit, mix, own_scr, sel, scr, p1, p2, pv,
           kf, kb, rb, tab, tab_sem, own_sem, fit_sem, orb_send, orb_recv, scr_send, scr_recv, out_send, out_recv):
    me, g = lax.axis_index("ka"), lax.axis_index("ga")
    e = lax.rem(me, 2)
    base = me - e
    width = fit_in.shape[2]
    tiles = width // tile
    bands = orb_in.shape[3]
    cond = bands - NV
    half = cond * cond

    barrier = pltpu.get_barrier_semaphore()
    count = 0
    for j in range(1, n):
        pl.semaphore_signal(barrier, inc=1, device_id=(lax.rem(me + j, n), g), device_id_type=MESH)
        count += 1
    for dg in range(ng - 1, 0, -1):
        for di in range(2):
            there = (base + lax.rem(e + di, 2), lax.rem(g + dg, ng))
            pl.semaphore_signal(barrier, inc=1, device_id=there, device_id_type=MESH)
            count += 1

    tab_copy = pltpu.make_async_copy(tab_in, tab, tab_sem)
    own_copy = pltpu.make_async_copy(scr_in.at[0], own_scr, own_sem)
    tab_copy.start()
    own_copy.start()
    fits = []
    for t in range(tiles):
        part = pl.ds(t * tile, tile)
        copy = pltpu.make_async_copy(fit_in.at[:, :, part], fit.at[:, :, part], fit_sem.at[t])
        copy.start()
        fits.append(copy)

    tab_copy.wait()
    own_copy.wait()
    for p in range(sel.shape[0]):
        row = jnp.zeros((1, width), jnp.float32)
        for q in range(own_scr.shape[0]):
            row = row + jnp.where(tab[p, 0] == q, 1.0, 0.0) * own_scr[q:q + 1]
        lines = [row[:, c * 128:(c + 1) * 128] for c in range(width // 128)]
        lines.append(jnp.zeros((sel.shape[1] - width // 128, 128), jnp.float32))
        sel[p] = jnp.concatenate([x for x in lines if x.shape[0]], 0).astype(LINK)
    pl.semaphore_wait(barrier, count)

    def screen_copy(s, j):
        return pltpu.make_async_remote_copy(
            src_ref=sel.at[lax.rem(e + j, 2)], dst_ref=scr.at[s], send_sem=scr_send.at[j - 1],
            recv_sem=scr_recv.at[s], device_id=(lax.rem(me + j, n), g), device_id_type=MESH)

    for s in range(STEPS):
        @pl.when(me == s + 1)
        def _():
            for j in range(1, n):
                screen_copy(s, j).start()
            pltpu.make_async_copy(sel.at[e], scr.at[s], scr_recv.at[s]).start()

    def orb_copy(h, d):
        there = lax.rem(base + 2 * h + d + n, n)
        return pltpu.make_async_remote_copy(
            src_ref=orb_in.at[:, 0], dst_ref=orb.at[2 * h + 1 - e], send_sem=orb_send.at[h, d],
            recv_sem=orb_recv.at[2 * h + 1 - e], device_id=(there, g), device_id_type=MESH)

    sends = [(h, d) for h in (1, 0, *range(2, (STEPS + 1) // 2 + 1)) for d in range(2)]

    def each_orb(act):
        for h, d in sends:
            if h == 1:
                act(orb_copy(h, d))
                continue

            @pl.when((e != d) if h == 0 else (2 * h + 1 - e <= STEPS + 1))
            def _():
                act(orb_copy(h, d))

    each_orb(lambda c: c.start())
    pltpu.make_async_copy(orb_in.at[:, 0], orb.at[1 - e], orb_recv.at[1 - e]).start()

    for t in range(tiles):
        fits[t].wait()
        part = slice(t * tile, (t + 1) * tile)
        x, y = fit[0, :, part].astype(jnp.float32), fit[1, :, part].astype(jnp.float32)
        mix[t, :, :tile] = (x + y).astype(jnp.bfloat16)
        mix[t, :, tile:] = (y - x).astype(jnp.bfloat16)

    def pair_products(s):
        for i in range(2):
            for a in range(2):
                b = lax.rem(a + e, 2)
                k = 2 * i + a
                home = orb[1 - i, :, a].astype(jnp.float32)
                far = orb[2 - i + s, :, b].astype(jnp.float32)
                cr, ci = pairs(home[0, NV:], home[1, NV:], far[0, NV:], far[1, NV:])
                both, less = (cr + ci).astype(jnp.bfloat16), (cr - ci).astype(jnp.bfloat16)
                low, high = slice(k * half, (k + 1) * half), slice((4 + k) * half, (5 + k) * half)
                p1[s, low], p1[s, high] = both, less
                p2[s, low], p2[s, high] = less, -both
                vr, vi = pairs(home[0, :NV], home[1, :NV], far[0, :NV], far[1, :NV])
                vr, vi = vr.astype(jnp.bfloat16), vi.astype(jnp.bfloat16)
                pv[s, i, 2 * a * half:(2 * a + 1) * half] = vr
                pv[s, i, (2 * a + 1) * half:(2 * a + 2) * half] = vi

    def out_copy(s, di, dg):
        i, gt = lax.rem(e + di, 2), lax.rem(g + dg, ng)
        return pltpu.make_async_remote_copy(
            src_ref=kb.at[s, i, gt], dst_ref=rb.at[s, di, dg], send_sem=out_send.at[s, di, dg],
            recv_sem=out_recv.at[s, di, dg], device_id=(base + i, gt), device_id_type=MESH)

    moves = [(di, dg) for dg in range(ng - 1, -1, -1) for di in range(2) if di or dg]
    def fold(s, t):
        part = slice(t * tile, (t + 1) * tile)
        each = tile // 128
        lines = scr[s].astype(jnp.float32)
        screen = jnp.concatenate([lines[t * each + c:t * each + c + 1] for c in range(each)], 1)
        xw = (fit[0, :, part].astype(jnp.float32) * screen).astype(jnp.bfloat16)
        yw = (fit[1, :, part].astype(jnp.float32) * screen).astype(jnp.bfloat16)
        return dot_nt(jnp.concatenate([xw, yw], 1), mix[t])

    def screen_wait(s):
        pltpu.make_async_copy(sel.at[e], scr.at[s], scr_recv.at[s]).wait()

    def folded(s, first, last, total=None):
        for t in range(first, last):
            total = fold(s, t) if total is None else total + fold(s, t)
        return (total * 0.5).astype(jnp.bfloat16) if last == tiles else total

    def applied(s, total):
        return (jnp.dot(p1[s], total, preferred_element_type=jnp.float32) + dot_nt(p2[s], total)).astype(jnp.bfloat16)

    sign = jnp.where(lax.broadcasted_iota(jnp.int32, (1, 2 * half), 1) < half, -1.0, 1.0)

    def finish(s, u):
        for i in range(2):
            ends = slice(2 * i * half, (2 * i + 2) * half), slice((2 * i + 4) * half, (2 * i + 6) * half)
            mixed = dot_nt(jnp.concatenate([u[ends[0]], u[ends[1]]], 0), pv[s, i])
            block = []
            for a in range(2):
                cols = slice(2 * a * half, (2 * a + 2) * half)
                by_imag = pltpu.roll(mixed[(2 + a) * half:(3 + a) * half, cols], half, 1)
                block.append(mixed[a * half:(a + 1) * half, cols] + by_imag * sign)
            block = jnp.concatenate(block, 0).reshape(kf.shape[2:])
            kf[s, i] = block
            kb[s, i] = block.astype(LINK)
        for t in range(ng - 1):
            up = jnp.where(t >= g, t + 1, t)
            down = jnp.where(ng - 1 - t <= g, ng - 2 - t, ng - 1 - t)
            gt = jnp.where(2 * g >= ng, up, down)
            dg = lax.rem(gt - g + ng, ng)
            for di in range(2):
                out_copy(s, di, dg).start()
        out_copy(s, 1, 0).start()

    order = range(STEPS)
    landed = set()

    def need(s):
        for j in sorted({0, 1, s + 1, s + 2} - landed):
            pltpu.make_async_copy(orb_in.at[:, 0], orb.at[j], orb_recv.at[j]).wait()
            landed.add(j)

    for s in order[:-1]:
        screen_wait(s)
    totals = {s: folded(s, 0, tiles) for s in order[:-1]}
    screen_wait(order[-1])
    for s in order:
        need(s)
    pair_products(order[0])
    u = applied(order[0], totals[order[0]])
    cut = min(3, tiles)
    last = folded(order[-1], 0, cut)
    finish(order[0], u)
    for s in order[1:]:
        pair_products(s)
    for s in order[1:-1]:
        u = applied(s, totals[s])
        if cut < tiles:
            last = folded(order[-1], cut, tiles, last)
        pass
        finish(s, u)
    u_last = applied(order[-1], last)
    finish(order[-1], u_last)

    rows = kf.shape[3]
    a_here = lax.div(g * rows, half)
    first = lax.rem(a_here + e, 2) == 0
    lane = lax.broadcasted_iota(jnp.int32, (rows, kf.shape[4]), 1)
    mid = kf.shape[4] // 2
    low = lane < mid
    for p, s in enumerate(order):
        if p == STEPS - 1:
            each_orb(lambda c: c.wait_send())
            for q in range(STEPS):
                @pl.when(me == q + 1)
                def _():
                    for j in range(1, n):
                        screen_copy(q, j).wait_send()
            for q in order[:-1]:
                for di, dg in moves:
                    out_copy(q, di, dg).wait_send()
        for di, dg in moves:
            out_copy(s, di, dg).wait_recv()
        own = kf[s, e, g]
        for dg in range(1, ng):
            own = own + rb[s, 0, dg].astype(jnp.float32)
        other = rb[s, 1, 0].astype(jnp.float32)
        for dg in range(1, ng):
            other = other + rb[s, 1, dg].astype(jnp.float32)
        b0 = jnp.where(first, own, other)
        b1 = jnp.where(first, other, own)
        out[0, s] = swapped(jnp.where(low, b0, pltpu.roll(b1, mid, 1)), NV)
        out[1, s] = swapped(jnp.where(low, pltpu.roll(b0, mid, 1), b1), NV)

    for di, dg in moves:
        out_copy(order[-1], di, dg).wait_send()


def body(orbitals, fit_vectors, screening, qpoint_table):
    n, ng = lax.axis_size("ka"), lax.axis_size("ga")
    _, _, kys, bands, points = orbitals.shape
    width = fit_vectors.shape[2]
    cond = bands - NV
    assert kys == 2 and cond == NV and n % 2 == 0 and n >= 2 * ((STEPS + 1) // 2 + 1)
    tile = next(t for t in (512, 384, 256, 128) if width % t == 0)
    rows = kys * cond * cond // ng
    wide = 2 * NV * NV
    lines = -(-width // 2048) * 16
    dma = pltpu.SemaphoreType.DMA
    any_spec = pl.BlockSpec(memory_space=pl.ANY)
    shares = pl.pallas_call(
        functools.partial(kernel, n, ng, tile),
        out_shape=pltpu.VMEM((2, STEPS, rows, wide), jnp.float32),
        in_specs=[any_spec] * 4,
        out_specs=pl.BlockSpec(memory_space=pltpu.VMEM),
        scratch_shapes=[
            pltpu.VMEM((STEPS + 2, 2, kys, bands, points), jnp.bfloat16),
            pltpu.VMEM((2, points, width), jnp.bfloat16),
            pltpu.VMEM((width // tile, points, 2 * tile), jnp.bfloat16),
            pltpu.VMEM((kys, width), jnp.float32),
            pltpu.VMEM((kys, lines, 128), LINK),
            pltpu.VMEM((STEPS, lines, 128), LINK),
            pltpu.VMEM((STEPS, 8 * cond * cond, points), jnp.bfloat16),
            pltpu.VMEM((STEPS, 8 * cond * cond, points), jnp.bfloat16),
            pltpu.VMEM((STEPS, 2, 2 * wide, points), jnp.bfloat16),
            pltpu.VMEM((STEPS, 2, ng, rows, wide), jnp.float32),
            pltpu.VMEM((STEPS, 2, ng, rows, wide), LINK),
            pltpu.VMEM((STEPS, 2, ng, rows, wide), LINK),
            pltpu.SMEM((kys, kys), jnp.int32),
            dma,
            dma,
            dma((width // tile,)),
            dma(((STEPS + 1) // 2 + 1, 2)),
            dma((STEPS + 2,)),
            dma((n - 1,)),
            dma((STEPS,)),
            dma((STEPS, 2, ng)),
            dma((STEPS, 2, ng)),
        ],
        compiler_params=pltpu.CompilerParams(collective_id=0, has_side_effects=True),
    )(orbitals, fit_vectors, screening, qpoint_table)
    return shares[:, :, None]


def solution(mesh):
    in_specs = (P(None, "ka", None, None, None), P(None, None, "ga"), P("ka", None, "ga"), P())
    out_specs = P(None, None, "ka", "ga", None)
    return jax.shard_map(body, mesh=mesh, in_specs=in_specs, out_specs=out_specs, check_vma=False)
```

```python
import functools
import jax
import jax.numpy as jnp
from jax import lax
from jax.experimental import pallas as pl
from jax.experimental.pallas import tpu as pltpu
from jax.sharding import PartitionSpec as P

NV = 8
STEPS = 3
MESH = pl.DeviceIdType.MESH
LINK = jnp.bfloat16


def dot_nt(a, b):
    return lax.dot_general(a, b, (((1,), (1,)), ((), ())), preferred_element_type=jnp.float32)


def pairs(ar, ai, br, bi):
    rows = ar.shape[0] * br.shape[0]
    ar, ai, br, bi = ar[:, None, :], ai[:, None, :], br[None], bi[None]
    real = (ar * br + ai * bi).reshape(rows, -1)
    imag = (ar * bi - ai * br).reshape(rows, -1)
    return real, imag


def swapped(x, size):
    row = lax.broadcasted_iota(jnp.int32, x.shape, 0)
    lane = lax.broadcasted_iota(jnp.int32, x.shape, 1)
    d = 1
    while d < size:
        rb = lax.rem(lax.div(row, d), 2)
        lb = lax.rem(lax.div(lane, d * size), 2)
        up = pltpu.roll(pltpu.roll(x, x.shape[0] - d, 0), d * size, 1)
        down = pltpu.roll(pltpu.roll(x, d, 0), x.shape[1] - d * size, 1)
        x = jnp.where(rb == lb, x, jnp.where(rb == 0, up, down))
        d *= 2
    return x


def kernel(n, ng, tile, orb_in, fit_in, scr_in, tab_in, out, orb, fit, mix, own_scr, sel, scr, p1, p2, pv,
           kf, kb, rb, tab, tab_sem, own_sem, fit_sem, orb_send, orb_recv, scr_send, scr_recv, out_send, out_recv):
    me, g = lax.axis_index("ka"), lax.axis_index("ga")
    e = lax.rem(me, 2)
    base = me - e
    width = fit_in.shape[2]
    tiles = width // tile
    bands = orb_in.shape[3]
    cond = bands - NV
    half = cond * cond

    barrier = pltpu.get_barrier_semaphore()
    count = 0
    for j in range(1, n):
        pl.semaphore_signal(barrier, inc=1, device_id=(lax.rem(me + j, n), g), device_id_type=MESH)
        count += 1
    for dg in range(ng - 1, 0, -1):
        for di in range(2):
            there = (base + lax.rem(e + di, 2), lax.rem(g + dg, ng))
            pl.semaphore_signal(barrier, inc=1, device_id=there, device_id_type=MESH)
            count += 1

    tab_copy = pltpu.make_async_copy(tab_in, tab, tab_sem)
    own_copy = pltpu.make_async_copy(scr_in.at[0], own_scr, own_sem)
    tab_copy.start()
    own_copy.start()
    fits = []
    for t in range(tiles):
        part = pl.ds(t * tile, tile)
        copy = pltpu.make_async_copy(fit_in.at[:, :, part], fit.at[:, :, part], fit_sem.at[t])
        copy.start()
        fits.append(copy)

    tab_copy.wait()
    own_copy.wait()
    for p in range(sel.shape[0]):
        row = jnp.zeros((1, width), jnp.float32)
        for q in range(own_scr.shape[0]):
            row = row + jnp.where(tab[p, 0] == q, 1.0, 0.0) * own_scr[q:q + 1]
        lines = [row[:, c * 128:(c + 1) * 128] for c in range(width // 128)]
        lines.append(jnp.zeros((sel.shape[1] - width // 128, 128), jnp.float32))
        sel[p] = jnp.concatenate([x for x in lines if x.shape[0]], 0).astype(LINK)
    pl.semaphore_wait(barrier, count)

    def screen_copy(s, j):
        return pltpu.make_async_remote_copy(
            src_ref=sel.at[lax.rem(e + j, 2)], dst_ref=scr.at[s], send_sem=scr_send.at[j - 1],
            recv_sem=scr_recv.at[s], device_id=(lax.rem(me + j, n), g), device_id_type=MESH)

    for s in range(STEPS):
        @pl.when(me == s + 1)
        def _():
            for j in [(d - s - 1) % n for d in range(n) if d != s + 1]:
                screen_copy(s, j).start()
            pltpu.make_async_copy(sel.at[e], scr.at[s], scr_recv.at[s]).start()

    def orb_copy(h, d):
        there = lax.rem(base + 2 * h + d + n, n)
        return pltpu.make_async_remote_copy(
            src_ref=orb_in.at[:, 0], dst_ref=orb.at[2 * h + 1 - e], send_sem=orb_send.at[h, d],
            recv_sem=orb_recv.at[2 * h + 1 - e], device_id=(there, g), device_id_type=MESH)

    sends = [(h, d) for h in (1, 0, *range(2, (STEPS + 1) // 2 + 1)) for d in range(2)]

    def each_orb(act):
        for h, d in sends:
            if h == 1:
                act(orb_copy(h, d))
                continue

            @pl.when((e != d) if h == 0 else (2 * h + 1 - e <= STEPS + 1))
            def _():
                act(orb_copy(h, d))

    each_orb(lambda c: c.start())
    pltpu.make_async_copy(orb_in.at[:, 0], orb.at[1 - e], orb_recv.at[1 - e]).start()

    for t in range(tiles):
        fits[t].wait()
        part = slice(t * tile, (t + 1) * tile)
        x, y = fit[0, :, part].astype(jnp.float32), fit[1, :, part].astype(jnp.float32)
        mix[t, :, :tile] = (x + y).astype(jnp.bfloat16)
        mix[t, :, tile:] = (y - x).astype(jnp.bfloat16)

    def pair_products(s):
        for i in range(2):
            for a in range(2):
                b = lax.rem(a + e, 2)
                k = 2 * i + a
                home = orb[1 - i, :, a].astype(jnp.float32)
                far = orb[2 - i + s, :, b].astype(jnp.float32)
                cr, ci = pairs(home[0, NV:], home[1, NV:], far[0, NV:], far[1, NV:])
                both, less = (cr + ci).astype(jnp.bfloat16), (cr - ci).astype(jnp.bfloat16)
                low, high = slice(k * half, (k + 1) * half), slice((4 + k) * half, (5 + k) * half)
                p1[s, low], p1[s, high] = both, less
                p2[s, low], p2[s, high] = less, -both
                vr, vi = pairs(home[0, :NV], home[1, :NV], far[0, :NV], far[1, :NV])
                vr, vi = vr.astype(jnp.bfloat16), vi.astype(jnp.bfloat16)
                pv[s, i, 2 * a * half:(2 * a + 1) * half] = vr
                pv[s, i, (2 * a + 1) * half:(2 * a + 2) * half] = vi

    def out_copy(s, di, dg):
        i, gt = lax.rem(e + di, 2), lax.rem(g + dg, ng)
        return pltpu.make_async_remote_copy(
            src_ref=kb.at[s, i, gt], dst_ref=rb.at[s, di, dg], send_sem=out_send.at[s, di, dg],
            recv_sem=out_recv.at[s, di, dg], device_id=(base + i, gt), device_id_type=MESH)

    moves = [(di, dg) for dg in range(ng - 1, -1, -1) for di in range(2) if di or dg]
    def fold(s, t):
        part = slice(t * tile, (t + 1) * tile)
        each = tile // 128
        lines = scr[s].astype(jnp.float32)
        screen = jnp.concatenate([lines[t * each + c:t * each + c + 1] for c in range(each)], 1)
        xw = (fit[0, :, part].astype(jnp.float32) * screen).astype(jnp.bfloat16)
        yw = (fit[1, :, part].astype(jnp.float32) * screen).astype(jnp.bfloat16)
        return dot_nt(jnp.concatenate([xw, yw], 1), mix[t])

    def screen_wait(s):
        pltpu.make_async_copy(sel.at[e], scr.at[s], scr_recv.at[s]).wait()

    def folded(s, first, last, total=None):
        for t in range(first, last):
            total = fold(s, t) if total is None else total + fold(s, t)
        return (total * 0.5).astype(jnp.bfloat16) if last == tiles else total

    def applied(s, total):
        return (jnp.dot(p1[s], total, preferred_element_type=jnp.float32) + dot_nt(p2[s], total)).astype(jnp.bfloat16)

    sign = jnp.where(lax.broadcasted_iota(jnp.int32, (1, 2 * half), 1) < half, -1.0, 1.0)

    def finish(s, u):
        for i in range(2):
            ends = slice(2 * i * half, (2 * i + 2) * half), slice((2 * i + 4) * half, (2 * i + 6) * half)
            mixed = dot_nt(jnp.concatenate([u[ends[0]], u[ends[1]]], 0), pv[s, i])
            block = []
            for a in range(2):
                cols = slice(2 * a * half, (2 * a + 2) * half)
                by_imag = pltpu.roll(mixed[(2 + a) * half:(3 + a) * half, cols], half, 1)
                block.append(mixed[a * half:(a + 1) * half, cols] + by_imag * sign)
            block = jnp.concatenate(block, 0).reshape(kf.shape[2:])
            kf[s, i] = block
            kb[s, i] = block.astype(LINK)

    def send(s, turns):
        for t in turns:
            up = jnp.where(t >= g, t + 1, t)
            down = jnp.where(ng - 1 - t <= g, ng - 2 - t, ng - 1 - t)
            gt = jnp.where(g > 0, up, down)
            dg = lax.rem(gt - g + ng, ng)
            for di in range(2):
                out_copy(s, di, dg).start()
        if turns[-1] == ng - 2:
            out_copy(s, 1, 0).start()

    order = range(STEPS)
    landed = set()

    def need(s):
        for j in sorted({0, 1, s + 1, s + 2} - landed):
            pltpu.make_async_copy(orb_in.at[:, 0], orb.at[j], orb_recv.at[j]).wait()
            landed.add(j)

    for s in order[:-1]:
        screen_wait(s)
    totals = {s: folded(s, 0, tiles) for s in order[:-1]}
    screen_wait(order[-1])
    for s in order:
        need(s)
    pair_products(order[0])
    u = applied(order[0], totals[order[0]])
    cut = max(1, tiles // 2)
    last = folded(order[-1], 0, cut)
    finish(order[0], u)
    send(order[0], range(ng - 1))
    for s in order[1:]:
        pair_products(s)
    for s in order[1:-1]:
        u = applied(s, totals[s])
        if cut < tiles:
            last = folded(order[-1], cut, tiles, last)
        finish(s, u)
        send(s, [0])
    u_last = applied(order[-1], last)
    finish(order[-1], u_last)
    send(order[-1], [0])
    for s in order[1:]:
        send(s, range(1, ng - 1))

    rows = kf.shape[3]
    a_here = lax.div(g * rows, half)
    first = lax.rem(a_here + e, 2) == 0
    lane = lax.broadcasted_iota(jnp.int32, (rows, kf.shape[4]), 1)
    mid = kf.shape[4] // 2
    low = lane < mid
    for p, s in enumerate(order):
        if p == STEPS - 1:
            each_orb(lambda c: c.wait_send())
            for q in range(STEPS):
                @pl.when(me == q + 1)
                def _():
                    for j in range(1, n):
                        screen_copy(q, j).wait_send()
            for q in order[:-1]:
                for di, dg in moves:
                    out_copy(q, di, dg).wait_send()
        for di, dg in moves:
            out_copy(s, di, dg).wait_recv()
        own = kf[s, e, g]
        for dg in range(1, ng):
            own = own + rb[s, 0, dg].astype(jnp.float32)
        other = rb[s, 1, 0].astype(jnp.float32)
        for dg in range(1, ng):
            other = other + rb[s, 1, dg].astype(jnp.float32)
        b0 = jnp.where(first, own, other)
        b1 = jnp.where(first, other, own)
        out[0, s] = swapped(jnp.where(low, b0, pltpu.roll(b1, mid, 1)), NV)
        out[1, s] = swapped(jnp.where(low, pltpu.roll(b0, mid, 1), b1), NV)

    for di, dg in moves:
        out_copy(order[-1], di, dg).wait_send()


def body(orbitals, fit_vectors, screening, qpoint_table):
    n, ng = lax.axis_size("ka"), lax.axis_size("ga")
    _, _, kys, bands, points = orbitals.shape
    width = fit_vectors.shape[2]
    cond = bands - NV
    assert kys == 2 and cond == NV and n % 2 == 0 and n >= 2 * ((STEPS + 1) // 2 + 1)
    tile = next(t for t in (512, 384, 256, 128) if width % t == 0)
    rows = kys * cond * cond // ng
    wide = 2 * NV * NV
    lines = -(-width // 2048) * 16
    dma = pltpu.SemaphoreType.DMA
    any_spec = pl.BlockSpec(memory_space=pl.ANY)
    shares = pl.pallas_call(
        functools.partial(kernel, n, ng, tile),
        out_shape=pltpu.VMEM((2, STEPS, rows, wide), jnp.float32),
        in_specs=[any_spec] * 4,
        out_specs=pl.BlockSpec(memory_space=pltpu.VMEM),
        scratch_shapes=[
            pltpu.VMEM((STEPS + 2, 2, kys, bands, points), jnp.bfloat16),
            pltpu.VMEM((2, points, width), jnp.bfloat16),
            pltpu.VMEM((width // tile, points, 2 * tile), jnp.bfloat16),
            pltpu.VMEM((kys, width), jnp.float32),
            pltpu.VMEM((kys, lines, 128), LINK),
            pltpu.VMEM((STEPS, lines, 128), LINK),
            pltpu.VMEM((STEPS, 8 * cond * cond, points), jnp.bfloat16),
            pltpu.VMEM((STEPS, 8 * cond * cond, points), jnp.bfloat16),
            pltpu.VMEM((STEPS, 2, 2 * wide, points), jnp.bfloat16),
            pltpu.VMEM((STEPS, 2, ng, rows, wide), jnp.float32),
            pltpu.VMEM((STEPS, 2, ng, rows, wide), LINK),
            pltpu.VMEM((STEPS, 2, ng, rows, wide), LINK),
            pltpu.SMEM((kys, kys), jnp.int32),
            dma,
            dma,
            dma((width // tile,)),
            dma(((STEPS + 1) // 2 + 1, 2)),
            dma((STEPS + 2,)),
            dma((n - 1,)),
            dma((STEPS,)),
            dma((STEPS, 2, ng)),
            dma((STEPS, 2, ng)),
        ],
        compiler_params=pltpu.CompilerParams(collective_id=0, has_side_effects=True),
    )(orbitals, fit_vectors, screening, qpoint_table)
    return shares[:, :, None]


def solution(mesh):
    in_specs = (P(None, "ka", None, None, None), P(None, None, "ga"), P("ka", None, "ga"), P())
    out_specs = P(None, None, "ka", "ga", None)
    return jax.shard_map(body, mesh=mesh, in_specs=in_specs, out_specs=out_specs, check_vma=False)
```

```python
import functools
import jax
import jax.numpy as jnp
from jax import lax
from jax.experimental import pallas as pl
from jax.experimental.pallas import tpu as pltpu
from jax.sharding import PartitionSpec as P

NV = 8
STEPS = 3
MESH = pl.DeviceIdType.MESH
LINK = jnp.bfloat16


def dot_nt(a, b):
    return lax.dot_general(a, b, (((1,), (1,)), ((), ())), preferred_element_type=jnp.float32)


def pairs(ar, ai, br, bi):
    rows = ar.shape[0] * br.shape[0]
    ar, ai, br, bi = ar[:, None, :], ai[:, None, :], br[None], bi[None]
    real = (ar * br + ai * bi).reshape(rows, -1)
    imag = (ar * bi - ai * br).reshape(rows, -1)
    return real, imag


def swapped(x, size):
    row = lax.broadcasted_iota(jnp.int32, x.shape, 0)
    lane = lax.broadcasted_iota(jnp.int32, x.shape, 1)
    d = 1
    while d < size:
        rb = lax.rem(lax.div(row, d), 2)
        lb = lax.rem(lax.div(lane, d * size), 2)
        up = pltpu.roll(pltpu.roll(x, x.shape[0] - d, 0), d * size, 1)
        down = pltpu.roll(pltpu.roll(x, d, 0), x.shape[1] - d * size, 1)
        x = jnp.where(rb == lb, x, jnp.where(rb == 0, up, down))
        d *= 2
    return x


def kernel(n, ng, tile, orb_in, fit_in, scr_in, tab_in, out, orb, fit, mix, own_scr, sel, scr, p1, p2, pv,
           kf, kb, rb, tab, tab_sem, own_sem, fit_sem, orb_send, orb_recv, scr_send, scr_recv, out_send, out_recv):
    me, g = lax.axis_index("ka"), lax.axis_index("ga")
    e = lax.rem(me, 2)
    base = me - e
    width = fit_in.shape[2]
    tiles = width // tile
    bands = orb_in.shape[3]
    cond = bands - NV
    half = cond * cond

    barrier = pltpu.get_barrier_semaphore()
    count = 0
    for j in range(1, n):
        pl.semaphore_signal(barrier, inc=1, device_id=(lax.rem(me + j, n), g), device_id_type=MESH)
        count += 1
    for dg in range(ng - 1, 0, -1):
        for di in range(2):
            there = (base + lax.rem(e + di, 2), lax.rem(g + dg, ng))
            pl.semaphore_signal(barrier, inc=1, device_id=there, device_id_type=MESH)
            count += 1

    tab_copy = pltpu.make_async_copy(tab_in, tab, tab_sem)
    own_copy = pltpu.make_async_copy(scr_in.at[0], own_scr, own_sem)
    tab_copy.start()
    own_copy.start()
    fits = []
    for t in range(tiles):
        part = pl.ds(t * tile, tile)
        copy = pltpu.make_async_copy(fit_in.at[:, :, part], fit.at[:, :, part], fit_sem.at[t])
        copy.start()
        fits.append(copy)

    tab_copy.wait()
    own_copy.wait()
    for p in range(sel.shape[0]):
        row = jnp.zeros((1, width), jnp.float32)
        for q in range(own_scr.shape[0]):
            row = row + jnp.where(tab[p, 0] == q, 1.0, 0.0) * own_scr[q:q + 1]
        lines = [row[:, c * 128:(c + 1) * 128] for c in range(width // 128)]
        lines.append(jnp.zeros((sel.shape[1] - width // 128, 128), jnp.float32))
        sel[p] = jnp.concatenate([x for x in lines if x.shape[0]], 0).astype(LINK)
    pl.semaphore_wait(barrier, count)

    def screen_copy(s, j):
        return pltpu.make_async_remote_copy(
            src_ref=sel.at[lax.rem(e + j, 2)], dst_ref=scr.at[s], send_sem=scr_send.at[j - 1],
            recv_sem=scr_recv.at[s], device_id=(lax.rem(me + j, n), g), device_id_type=MESH)

    for s in range(STEPS):
        @pl.when(me == s + 1)
        def _():
            for j in [(d - s - 1) % n for d in range(n) if d != s + 1]:
                screen_copy(s, j).start()
            pltpu.make_async_copy(sel.at[e], scr.at[s], scr_recv.at[s]).start()

    def orb_copy(h, d):
        there = lax.rem(base + 2 * h + d + n, n)
        return pltpu.make_async_remote_copy(
            src_ref=orb_in.at[:, 0], dst_ref=orb.at[2 * h + 1 - e], send_sem=orb_send.at[h, d],
            recv_sem=orb_recv.at[2 * h + 1 - e], device_id=(there, g), device_id_type=MESH)

    sends = [(h, d) for h in (1, 0, *range(2, (STEPS + 1) // 2 + 1)) for d in range(2)]

    def each_orb(act):
        for h, d in sends:
            if h == 1:
                act(orb_copy(h, d))
                continue

            @pl.when((e != d) if h == 0 else (2 * h + 1 - e <= STEPS + 1))
            def _():
                act(orb_copy(h, d))

    each_orb(lambda c: c.start())
    pltpu.make_async_copy(orb_in.at[:, 0], orb.at[1 - e], orb_recv.at[1 - e]).start()

    for t in range(tiles):
        fits[t].wait()
        part = slice(t * tile, (t + 1) * tile)
        x, y = fit[0, :, part].astype(jnp.float32), fit[1, :, part].astype(jnp.float32)
        mix[t, :, :tile] = (x + y).astype(jnp.bfloat16)
        mix[t, :, tile:] = (y - x).astype(jnp.bfloat16)

    def pair_products(s):
        for i in range(2):
            for a in range(2):
                b = lax.rem(a + e, 2)
                k = 2 * i + a
                home = orb[1 - i, :, a].astype(jnp.float32)
                far = orb[2 - i + s, :, b].astype(jnp.float32)
                cr, ci = pairs(home[0, NV:], home[1, NV:], far[0, NV:], far[1, NV:])
                both, less = (cr + ci).astype(jnp.bfloat16), (cr - ci).astype(jnp.bfloat16)
                low, high = slice(k * half, (k + 1) * half), slice((4 + k) * half, (5 + k) * half)
                p1[s, low], p1[s, high] = both, less
                p2[s, low], p2[s, high] = less, -both
                vr, vi = pairs(home[0, :NV], home[1, :NV], far[0, :NV], far[1, :NV])
                vr, vi = vr.astype(jnp.bfloat16), vi.astype(jnp.bfloat16)
                pv[s, i, 2 * a * half:(2 * a + 1) * half] = vr
                pv[s, i, (2 * a + 1) * half:(2 * a + 2) * half] = vi

    def out_copy(s, di, dg):
        i, gt = lax.rem(e + di, 2), lax.rem(g + dg, ng)
        return pltpu.make_async_remote_copy(
            src_ref=kb.at[s, i, gt], dst_ref=rb.at[s, di, dg], send_sem=out_send.at[s, di, dg],
            recv_sem=out_recv.at[s, di, dg], device_id=(base + i, gt), device_id_type=MESH)

    moves = [(di, dg) for dg in range(ng - 1, -1, -1) for di in range(2) if di or dg]
    def fold(s, t):
        part = slice(t * tile, (t + 1) * tile)
        each = tile // 128
        lines = scr[s].astype(jnp.float32)
        screen = jnp.concatenate([lines[t * each + c:t * each + c + 1] for c in range(each)], 1)
        xw = (fit[0, :, part].astype(jnp.float32) * screen).astype(jnp.bfloat16)
        yw = (fit[1, :, part].astype(jnp.float32) * screen).astype(jnp.bfloat16)
        return dot_nt(jnp.concatenate([xw, yw], 1), mix[t])

    def screen_wait(s):
        pltpu.make_async_copy(sel.at[e], scr.at[s], scr_recv.at[s]).wait()

    def folded(s, first, last, total=None):
        for t in range(first, last):
            total = fold(s, t) if total is None else total + fold(s, t)
        return (total * 0.5).astype(jnp.bfloat16) if last == tiles else total

    def applied(s, total):
        return (jnp.dot(p1[s], total, preferred_element_type=jnp.float32) + dot_nt(p2[s], total)).astype(jnp.bfloat16)

    sign = jnp.where(lax.broadcasted_iota(jnp.int32, (1, 2 * half), 1) < half, -1.0, 1.0)

    def finish(s, u):
        for i in range(2):
            ends = slice(2 * i * half, (2 * i + 2) * half), slice((2 * i + 4) * half, (2 * i + 6) * half)
            mixed = dot_nt(jnp.concatenate([u[ends[0]], u[ends[1]]], 0), pv[s, i])
            block = []
            for a in range(2):
                cols = slice(2 * a * half, (2 * a + 2) * half)
                by_imag = pltpu.roll(mixed[(2 + a) * half:(3 + a) * half, cols], half, 1)
                block.append(mixed[a * half:(a + 1) * half, cols] + by_imag * sign)
            block = jnp.concatenate(block, 0).reshape(kf.shape[2:])
            kf[s, i] = block
            kb[s, i] = block.astype(LINK)

    def send(s, turns):
        for t in turns:
            up = jnp.where(t >= g, t + 1, t)
            down = jnp.where(ng - 1 - t <= g, ng - 2 - t, ng - 1 - t)
            gt = jnp.where(g > 0, up, down)
            dg = lax.rem(gt - g + ng, ng)
            for di in range(2):
                out_copy(s, di, dg).start()
        if turns[-1] == ng - 2:
            out_copy(s, 1, 0).start()

    order = range(STEPS)
    landed = set()

    def need(s):
        for j in sorted({0, 1, s + 1, s + 2} - landed):
            pltpu.make_async_copy(orb_in.at[:, 0], orb.at[j], orb_recv.at[j]).wait()
            landed.add(j)

    totals = {}
    for s in order[:-1]:
        screen_wait(s)
        totals[s] = folded(s, 0, tiles)
    screen_wait(order[-1])
    for s in order:
        need(s)
    pair_products(order[0])
    u = applied(order[0], totals[order[0]])
    cut = max(1, tiles // 2)
    last = folded(order[-1], 0, cut)
    finish(order[0], u)
    send(order[0], range(ng - 1))
    for s in order[1:]:
        pair_products(s)
    for s in order[1:-1]:
        u = applied(s, totals[s])
        if cut < tiles:
            last = folded(order[-1], cut, tiles, last)
        finish(s, u)
        send(s, [0])
    u_last = applied(order[-1], last)
    finish(order[-1], u_last)
    send(order[-1], [0])
    for s in order[1:]:
        send(s, range(1, ng - 1))

    rows = kf.shape[3]
    a_here = lax.div(g * rows, half)
    first = lax.rem(a_here + e, 2) == 0
    lane = lax.broadcasted_iota(jnp.int32, (rows, kf.shape[4]), 1)
    mid = kf.shape[4] // 2
    low = lane < mid
    for p, s in enumerate(order):
        if p == STEPS - 1:
            each_orb(lambda c: c.wait_send())
            for q in range(STEPS):
                @pl.when(me == q + 1)
                def _():
                    for j in range(1, n):
                        screen_copy(q, j).wait_send()
            for q in order[:-1]:
                for di, dg in moves:
                    out_copy(q, di, dg).wait_send()
        for di, dg in moves:
            out_copy(s, di, dg).wait_recv()
        own = kf[s, e, g]
        for dg in range(1, ng):
            own = own + rb[s, 0, dg].astype(jnp.float32)
        other = rb[s, 1, 0].astype(jnp.float32)
        for dg in range(1, ng):
            other = other + rb[s, 1, dg].astype(jnp.float32)
        b0 = jnp.where(first, own, other)
        b1 = jnp.where(first, other, own)
        out[0, s] = swapped(jnp.where(low, b0, pltpu.roll(b1, mid, 1)), NV)
        out[1, s] = swapped(jnp.where(low, pltpu.roll(b0, mid, 1), b1), NV)

    for di, dg in moves:
        out_copy(order[-1], di, dg).wait_send()


def body(orbitals, fit_vectors, screening, qpoint_table):
    n, ng = lax.axis_size("ka"), lax.axis_size("ga")
    _, _, kys, bands, points = orbitals.shape
    width = fit_vectors.shape[2]
    cond = bands - NV
    assert kys == 2 and cond == NV and n % 2 == 0 and n >= 2 * ((STEPS + 1) // 2 + 1)
    tile = next(t for t in (512, 384, 256, 128) if width % t == 0)
    rows = kys * cond * cond // ng
    wide = 2 * NV * NV
    lines = -(-width // 2048) * 16
    dma = pltpu.SemaphoreType.DMA
    any_spec = pl.BlockSpec(memory_space=pl.ANY)
    shares = pl.pallas_call(
        functools.partial(kernel, n, ng, tile),
        out_shape=pltpu.VMEM((2, STEPS, rows, wide), jnp.float32),
        in_specs=[any_spec] * 4,
        out_specs=pl.BlockSpec(memory_space=pltpu.VMEM),
        scratch_shapes=[
            pltpu.VMEM((STEPS + 2, 2, kys, bands, points), jnp.bfloat16),
            pltpu.VMEM((2, points, width), jnp.bfloat16),
            pltpu.VMEM((width // tile, points, 2 * tile), jnp.bfloat16),
            pltpu.VMEM((kys, width), jnp.float32),
            pltpu.VMEM((kys, lines, 128), LINK),
            pltpu.VMEM((STEPS, lines, 128), LINK),
            pltpu.VMEM((STEPS, 8 * cond * cond, points), jnp.bfloat16),
            pltpu.VMEM((STEPS, 8 * cond * cond, points), jnp.bfloat16),
            pltpu.VMEM((STEPS, 2, 2 * wide, points), jnp.bfloat16),
            pltpu.VMEM((STEPS, 2, ng, rows, wide), jnp.float32),
            pltpu.VMEM((STEPS, 2, ng, rows, wide), LINK),
            pltpu.VMEM((STEPS, 2, ng, rows, wide), LINK),
            pltpu.SMEM((kys, kys), jnp.int32),
            dma,
            dma,
            dma((width // tile,)),
            dma(((STEPS + 1) // 2 + 1, 2)),
            dma((STEPS + 2,)),
            dma((n - 1,)),
            dma((STEPS,)),
            dma((STEPS, 2, ng)),
            dma((STEPS, 2, ng)),
        ],
        compiler_params=pltpu.CompilerParams(collective_id=0, has_side_effects=True),
    )(orbitals, fit_vectors, screening, qpoint_table)
    return shares[:, :, None]


def solution(mesh):
    in_specs = (P(None, "ka", None, None, None), P(None, None, "ga"), P("ka", None, "ga"), P())
    out_specs = P(None, None, "ka", "ga", None)
    return jax.shard_map(body, mesh=mesh, in_specs=in_specs, out_specs=out_specs, check_vma=False)
```
